32 devices in a mesh: row: 16 (over z, y, x), rep: 2 (over core).
Axes of the slice: x: 2, y: 2, z: 4, core: 2. Of those that a mesh axis runs over, the one named last changes fastest.
Arguments:
- node_feats: bfloat16 [4096, 256], P(('row', 'rep')), may hold values from -6 to 6
- edge_feats: bfloat16 [32768, 256], P(('row', 'rep')), may hold values from -6 to 6
- senders: int32 [32768], P(('row', 'rep')), may hold values from 0 to 4095, as said below
- receivers: int32 [32768], P(('row', 'rep')), may hold values from 0 to 4095, as said below
- edge_count: int32 [32], P(('row', 'rep')), may hold values from 512 to 1024, as said below
- w_edge_in: bfloat16 [768, 256], replicated, may hold values from -0.21875 to 0.21875
- w_edge_out: bfloat16 [256, 256], replicated, may hold values from -0.375 to 0.375
- gain_edge: float32 [256], replicated, may hold values from 0.5 to 2
- w_node_in: bfloat16 [512, 256], replicated, may hold values from -0.25 to 0.25
- w_node_out: bfloat16 [256, 256], replicated, may hold values from -0.375 to 0.375
- gain_node: float32 [256], replicated, may hold values from 0.5 to 2
- d_nodes_out: bfloat16 [4096, 256], P(('row', 'rep')), may hold values from -6 to 6
- d_edges_out: bfloat16 [32768, 256], P(('row', 'rep')), may hold values from -6 to 6
Outputs:
- nodes_out: bfloat16 [4096, 256], P(('row', 'rep'))
- edges_out: bfloat16 [32768, 256], P(('row', 'rep'))
- d_nodes: bfloat16 [4096, 256], P(('row', 'rep'))
- d_edges: bfloat16 [32768, 256], P(('row', 'rep'))
- d_w_edge_in: bfloat16 [768, 256], replicated
- d_w_edge_out: bfloat16 [256, 256], replicated
- d_gain_edge: float32 [256], replicated
- d_w_node_in: bfloat16 [512, 256], replicated
- d_w_node_out: bfloat16 [256, 256], replicated
- d_gain_node: float32 [256], replicated
The draws below stay inside these ranges and needn't reach their ends.
Inputs may be any that keep to these rules, and one draw needn't show every extreme that they name: `receivers`: edge i's receiver lies in nodes g * 256 to (g + 1) * 256 - 1 with g = i // 2048. `senders`: an edge's sender differs from its receiver by at most 128; in every aligned block of 1024 edge slots some edge reaches 128. The first edge_count[k] slots of the k-th aligned block of 1024 slots are live; some block is full.
All inputs are finite; a program needn't handle non-finite values.
Results may differ from the reference program's by a relative error of at most 0.013.
Values may be sent and summed in bfloat16 or wider, within the bound.
A program may use at most 64 MiB of HBM per device.

```python
import math
import jax
import jax.numpy as jnp
from jax import lax

D = 256
GROUP = 256
RIM = 128
NODES = 4096
EDGE_DEV = 1024
EDGES = 32768
N_ROW = 16
N_REP = 2


def edge_graph(key):
    graph_key = jax.random.fold_in(key, 7)
    key_recv, key_span, key_sign = jax.random.split(graph_key, 3)
    slots = jnp.arange(EDGES, dtype=jnp.int32)
    device_id = slots // EDGE_DEV
    group_id = device_id // N_REP
    receivers = group_id * GROUP + jax.random.randint(key_recv, (EDGES,), 0, GROUP, dtype=jnp.int32)
    spans = jax.random.randint(key_span, (EDGES,), 1, RIM + 1, dtype=jnp.int32)
    signs = 2 * jax.random.randint(key_sign, (EDGES,), 0, 2, dtype=jnp.int32) - 1
    first_slot = slots % EDGE_DEV == 0
    spans = jnp.where(first_slot, RIM, spans)
    signs = jnp.where(first_slot, jnp.where(group_id < N_ROW - 1, 1, -1), signs)
    senders = jnp.clip(receivers + signs * spans, 0, NODES - 1)
    return (senders.astype(jnp.int32), receivers.astype(jnp.int32))


def draw_senders(key, part):
    return edge_graph(key)[0]


def draw_receivers(key, part):
    return edge_graph(key)[1]


def draw_edge_count(key, part):
    count_key = jax.random.fold_in(key, 11)
    key_count, key_full = jax.random.split(count_key, 2)
    blocks = N_ROW * N_REP
    counts = jax.random.randint(key_count, (blocks,), EDGE_DEV // 2, EDGE_DEV + 1, dtype=jnp.int32)
    full_block = jax.random.randint(key_full, (), 0, blocks, dtype=jnp.int32)
    return jnp.where(jnp.arange(blocks, dtype=jnp.int32) == full_block, EDGE_DEV, counts).astype(jnp.int32)


def raised(result, key, source, target, shards_of, factor):
    owner, partner = [(jnp.arange(result.shape[dim]) // (result.shape[dim] // shards_of)).reshape([-1 if axis == dim else 1 for axis in range(result.ndim)]) for dim in (source, target)]
    chosen = jax.random.permutation(key, shards_of)[partner]
    strong = (owner == chosen) | (owner == (partner + shards_of // 2) % shards_of)
    return jnp.where(strong, factor * result, result)


def steps_of(key, extent, pieces, smallest, largest):
    def one(axis_at, blocks):
        draws = jax.random.uniform(jax.random.fold_in(jax.random.fold_in(key, 6), axis_at), (blocks,), jnp.float32, smallest / len(pieces), largest / len(pieces))
        return jnp.repeat(jnp.exp(draws), extent[axis_at] // blocks).reshape((-1,) + (1,) * (len(extent) - axis_at - 1))

    loudness = one(*pieces[0])
    for cut in pieces[1:]:
        loudness = loudness * one(*cut)
    return loudness


def bell_draw(key, dims, spread, reach, cuts=(), held_as=jnp.bfloat16):
    array = spread * jax.random.normal(key, dims, jnp.float32)
    if cuts:
        array = array * steps_of(key, dims, cuts, -0.22, 0.18)
    return jnp.clip(array, -reach, reach).astype(held_as)


def gaussian_with(stream_key, dims, deviation, bound, shards, heavy, held_as=jnp.bfloat16):
    entries = deviation * jax.random.normal(stream_key, dims, jnp.float32)
    if shards:
        entries = entries * steps_of(stream_key, dims, shards, -0.22, 0.18)
    return jnp.clip(raised(entries, jax.random.fold_in(stream_key, 3), *heavy), -bound, bound).astype(held_as)


def setup_inputs(seed: int = 0) -> dict:
    seeds = jax.random.split(jax.random.key(seed), 14)
    node_feats = bell_draw(seeds[0], (NODES, D), 1.0, 6.0, ((0, 32),))
    edge_feats = bell_draw(seeds[1], (EDGES, D), 1.0, 6.0, ((0, 32),))
    senders = draw_senders(jax.random.fold_in(seeds[13], 71), 0)
    receivers = draw_receivers(jax.random.fold_in(seeds[13], 71), 0)
    edge_count = draw_edge_count(jax.random.fold_in(seeds[13], 71), 0)
    w_edge_in = bell_draw(seeds[5], (3 * D, D), (3 * D) ** -0.5, 0.21875)
    w_edge_out = bell_draw(seeds[6], (D, D), D ** -0.5, 0.375)
    gain_edge = jnp.clip(jnp.exp(jax.random.uniform(seeds[7], (D,), jnp.float32, math.log(0.5), math.log(2.0))), 0.5, 2.0)
    w_node_in = bell_draw(seeds[8], (2 * D, D), (2 * D) ** -0.5, 0.25)
    w_node_out = bell_draw(seeds[9], (D, D), D ** -0.5, 0.375)
    gain_node = jnp.clip(jnp.exp(jax.random.uniform(seeds[10], (D,), jnp.float32, math.log(0.5), math.log(2.0))), 0.5, 2.0)
    d_nodes_out = gaussian_with(seeds[11], (NODES, D), 1.0, 6.0, ((0, 32),), (0, 1, 32, 2.75))
    d_edges_out = gaussian_with(seeds[12], (EDGES, D), 1.0, 6.0, ((0, 32),), (0, 1, 32, 2.75))
    return {"node_feats": node_feats, "edge_feats": edge_feats, "senders": senders, "receivers": receivers, "edge_count": edge_count, "w_edge_in": w_edge_in, "w_edge_out": w_edge_out, "gain_edge": gain_edge, "w_node_in": w_node_in, "w_node_out": w_node_out, "gain_node": gain_node, "d_nodes_out": d_nodes_out, "d_edges_out": d_edges_out}


def silu_slope(pre):
    sigmoid = jax.nn.sigmoid(pre)
    return sigmoid * (1.0 + pre * (1.0 - sigmoid))

def layer_norm(values):
    centred = values - lax.optimization_barrier(jnp.mean(values, axis=-1, keepdims=True))
    inv_scale = lax.rsqrt(lax.optimization_barrier(jnp.mean(centred * centred, axis=-1, keepdims=True)) + 1e-05)
    return (centred * inv_scale, inv_scale)

def norm_back(upstream, normed, inv_scale):
    return inv_scale * (upstream - lax.optimization_barrier(jnp.mean(upstream, axis=-1, keepdims=True)) - normed * lax.optimization_barrier(jnp.mean(upstream * normed, axis=-1, keepdims=True)))

def contract_rows(left, right):
    return lax.dot_general(left, right, (((0,), (0,)), ((), ())), preferred_element_type=jnp.float32)

def times_transpose(left, right):
    return lax.dot_general(left, right, (((1,), (1,)), ((), ())), preferred_element_type=jnp.float32)

def widen(values):
    return lax.optimization_barrier(values).astype(jnp.float32)

def reference(node_feats, edge_feats, senders, receivers, edge_count, w_edge_in, w_edge_out, gain_edge, w_node_in, w_node_out, gain_node, d_nodes_out, d_edges_out):
    slots = jnp.arange(EDGES, dtype=jnp.int32)
    live_mask = (slots % EDGE_DEV < edge_count[slots // EDGE_DEV]).astype(jnp.float32)[:, None]
    edge_input = jnp.concatenate([edge_feats, node_feats[senders], node_feats[receivers]], axis=1)
    edge_pre = jnp.dot(edge_input, w_edge_in, preferred_element_type=jnp.float32)
    edge_act = jax.nn.silu(edge_pre).astype(jnp.bfloat16)
    edge_mix = jnp.dot(edge_act, w_edge_out, preferred_element_type=jnp.float32)
    edge_norm, edge_scale = layer_norm(edge_mix)
    message = live_mask * edge_norm * gain_edge
    edges_out = (edge_feats.astype(jnp.float32) + message).astype(jnp.bfloat16)
    message_b = message.astype(jnp.bfloat16)
    aggregate = jax.ops.segment_sum(widen(message_b), receivers, num_segments=NODES)
    node_input = jnp.concatenate([node_feats, aggregate.astype(jnp.bfloat16)], axis=1)
    node_pre = jnp.dot(node_input, w_node_in, preferred_element_type=jnp.float32)
    node_act = jax.nn.silu(node_pre).astype(jnp.bfloat16)
    node_mix = jnp.dot(node_act, w_node_out, preferred_element_type=jnp.float32)
    node_norm, node_scale = layer_norm(node_mix)
    nodes_out = (node_feats.astype(jnp.float32) + node_norm * gain_node).astype(jnp.bfloat16)
    grad_nodes = d_nodes_out.astype(jnp.float32)
    d_gain_node = lax.optimization_barrier(jnp.sum(grad_nodes * node_norm, axis=0))
    d_node_mix = norm_back(grad_nodes * gain_node, node_norm, node_scale).astype(jnp.bfloat16)
    d_w_node_out = contract_rows(node_act, d_node_mix).astype(jnp.bfloat16)
    d_node_pre = (times_transpose(d_node_mix, w_node_out) * silu_slope(node_pre)).astype(jnp.bfloat16)
    d_w_node_in = contract_rows(node_input, d_node_pre).astype(jnp.bfloat16)
    d_node_input = times_transpose(d_node_pre, w_node_in)
    d_aggregate = d_node_input[:, D:].astype(jnp.bfloat16)
    d_message = live_mask * (d_edges_out.astype(jnp.float32) + d_aggregate[receivers].astype(jnp.float32))
    d_gain_edge = lax.optimization_barrier(jnp.sum(d_message * edge_norm, axis=0))
    d_edge_mix = norm_back(d_message * gain_edge, edge_norm, edge_scale).astype(jnp.bfloat16)
    d_w_edge_out = contract_rows(edge_act, d_edge_mix).astype(jnp.bfloat16)
    d_edge_pre = (times_transpose(d_edge_mix, w_edge_out) * silu_slope(edge_pre)).astype(jnp.bfloat16)
    d_w_edge_in = contract_rows(edge_input, d_edge_pre).astype(jnp.bfloat16)
    d_edge_input = times_transpose(d_edge_pre, w_edge_in)
    d_edges = (d_edges_out.astype(jnp.float32) + d_edge_input[:, :D]).astype(jnp.bfloat16)
    d_sender = d_edge_input[:, D:2 * D].astype(jnp.bfloat16)
    d_receiver = d_edge_input[:, 2 * D:].astype(jnp.bfloat16)
    from_edges = jax.ops.segment_sum(widen(d_sender), senders, num_segments=NODES)
    from_edges = from_edges + jax.ops.segment_sum(widen(d_receiver), receivers, num_segments=NODES)
    d_nodes = (grad_nodes + d_node_input[:, :D] + from_edges).astype(jnp.bfloat16)
    return (nodes_out, edges_out, d_nodes, d_edges, d_w_edge_in, d_w_edge_out, d_gain_edge, d_w_node_in, d_w_node_out, d_gain_node)
```

```python
import functools

import jax
import jax.numpy as jnp
from jax import lax
from jax.experimental import pallas as pl
from jax.experimental.pallas import tpu as pltpu
from jax.sharding import PartitionSpec as P

F32 = jnp.float32
BF16 = jnp.bfloat16
LANES = 128
MESH = pl.DeviceIdType.MESH


def mm(left, right):
    return jnp.dot(left, right, preferred_element_type=F32)


def contract_rows(left, right):
    return lax.dot_general(left, right, (((0,), (0,)), ((), ())), preferred_element_type=F32)


def times_transpose(left, right):
    return lax.dot_general(left, right, (((1,), (1,)), ((), ())), preferred_element_type=F32)


def sigmoid(v):
    return 1.0 / (1.0 + jnp.exp(-v))


def layer_norm(values):
    centred = values - jnp.mean(values, axis=-1, keepdims=True)
    inv_scale = lax.rsqrt(jnp.mean(centred * centred, axis=-1, keepdims=True) + 1e-05)
    return (centred * inv_scale, inv_scale)


def norm_back(upstream, normed, inv_scale):
    return inv_scale * (
        upstream
        - jnp.mean(upstream, axis=-1, keepdims=True)
        - normed * jnp.mean(upstream * normed, axis=-1, keepdims=True)
    )


def digits_of(n_row):
    out, stride = [], 1
    while stride < n_row:
        radix = 4 if n_row % (stride * 4) == 0 else 2
        out.append((stride, radix))
        stride *= radix
    return out


def tree(values):
    while len(values) > 1:
        values = [values[i] + values[i + 1] for i in range(0, len(values), 2)]
    return values[0]


class Reduction:
    def __init__(self, rank, digits, buf, recv_rep, recvs, gathered, sends, sems):
        self.row, self.rep, self.digits = rank[0], rank[1], digits
        self.buf, self.recv_rep, self.recvs, self.gathered = buf, recv_rep, recvs, gathered
        self.send, self.recv = sends, sems
        self.mine = [(self.row // s) % r for s, r in digits]
        self.live = []
        self.slot = 0

    def partner(self, level, k):
        stride, _ = self.digits[level]
        d = self.mine[level]
        other = jnp.bitwise_xor(d, k)
        return self.row + (other - d) * stride, other

    def copy(self, src, dst, device):
        c = pltpu.make_async_remote_copy(
            src_ref=src,
            dst_ref=dst,
            send_sem=self.send.at[self.slot],
            recv_sem=self.recv.at[self.slot],
            device_id=device,
            device_id_type=MESH,
        )
        self.slot += 1
        c.start()
        self.live.append(c)

    def wait(self):
        for c in self.live:
            c.wait()
        self.live = []

    def start_rep(self):
        self.copy(self.buf.at[1 - self.rep], self.recv_rep, (self.row, 1 - self.rep))

    def at(self, ref, level):
        for d in self.mine[:level]:
            ref = ref.at[d]
        return ref

    def add_rep(self):
        self.wait()
        self.buf[self.rep] = (self.buf[self.rep].astype(F32) + self.recv_rep[...].astype(F32)).astype(BF16)

    def start_level(self, level):
        ref = self.at(self.buf.at[self.rep], level)
        for k in range(1, self.digits[level][1]):
            row, other = self.partner(level, k)
            self.copy(ref.at[other], self.recvs[level].at[k - 1], (row, self.rep))

    def add_level(self, level):
        self.wait()
        ref = self.at(self.buf.at[self.rep], level + 1)
        parts = [ref[...].astype(F32)]
        parts += [self.recvs[level][k].astype(F32) for k in range(self.digits[level][1] - 1)]
        total = tree(parts).astype(BF16)
        if level + 1 == len(self.digits):
            self.at(self.gathered.at[self.rep], level + 1)[...] = total
        else:
            ref[...] = total

    def start_gather(self, level):
        ref = self.at(self.gathered.at[self.rep], level + 1)
        for k in range(1, self.digits[level][1]):
            row, _ = self.partner(level, k)
            self.copy(ref, ref, (row, self.rep))

    def start_gather_rep(self):
        self.copy(self.gathered.at[self.rep], self.gathered.at[self.rep], (self.row, 1 - self.rep))

    def put(self, array, first):
        block = self.buf.shape[-2]
        _ = first
        for h in range(2):
            part = array[:, h * LANES : (h + 1) * LANES].astype(BF16)
            self.buf[h] = part.reshape(self.buf.shape[1:])

    def take(self, h):
        full = self.gathered[h]
        return full.reshape((-1, LANES))


def kernel(
    digits,
    n_row,
    chunk,
    nf_ref, ef_ref, send_ref, recv_ref, count_ref,
    wei_ref, weo_ref, ge_ref, wni_ref, wno_ref, gn_ref, dn_ref, de_ref,
    nodes_out, edges_out, d_nodes, d_edges, o_wei, o_weo, o_ge, o_wni, o_wno, o_gn,
    ext, table, cols, pre_s, norm_s, scale_s, act_s, psum, psum_in, grp_grad,
    s_sum, r_sum, dwe, dwo, big_e, big_n, halo_out, halo_in, sib_out, sib_in,
    gains, gains_in,
    buf_n, rep_n, gat_n, buf_e, rep_e, gat_e,
    send_sem, recv_sem, nsend, nrecv, esend, erecv, gsend, grecv,
    *level_refs,
):
    row, rep = lax.axis_index("row"), lax.axis_index("rep")
    sib = 1 - rep
    shard, width = nf_ref.shape
    edges = ef_ref.shape[0]
    n_chunks = edges // chunk
    levels = len(digits)
    has_prev, has_next = row > 0, row < n_row - 1
    red_n = Reduction((row, rep), digits, buf_n, rep_n, level_refs[:levels], gat_n, nsend, nrecv)
    red_e = Reduction((row, rep), digits, buf_e, rep_e, level_refs[levels:], gat_e, esend, erecv)

    def remote(src, dst, slot, device, there=None):
        return pltpu.make_async_remote_copy(
            src_ref=src, dst_ref=dst, send_sem=send_sem.at[slot],
            recv_sem=recv_sem.at[slot if there is None else there],
            device_id=device, device_id_type=MESH,
        )

    barrier = pltpu.get_barrier_semaphore()

    def greet(device):
        pl.semaphore_signal(barrier, inc=1, device_id=device, device_id_type=MESH)

    greet((row, sib))
    level_partners = 0
    for level, (_, radix) in enumerate(digits):
        for k in range(1, radix):
            greet((red_n.partner(level, k)[0], rep))
            level_partners += 1

    @pl.when(has_prev)
    def _():
        for r in range(2):
            greet((row - 1, r))

    @pl.when(has_next)
    def _():
        for r in range(2):
            greet((row + 1, r))

    around = 2 * (jnp.int32(has_prev) + jnp.int32(has_next))
    pl.semaphore_wait(barrier, 1 + level_partners + around)

    own = 1 + rep
    to_sib = remote(nf_ref, ext.at[own], 0, (row, sib))
    to_sib.start()
    goes = ((rep == 0) & has_prev) | ((rep == 1) & has_next)
    target = jnp.where(rep == 0, row - 1, row + 1)
    place = jnp.where(rep == 0, 3, 0)

    def halo_copy(r):
        return remote(nf_ref, ext.at[place], 1 + r, (target, r), there=jnp.where(rep == 0, 4, 3))

    @pl.when(goes)
    def _():
        for r in range(2):
            halo_copy(r).start()

    ext[own] = nf_ref[...]

    @pl.when(jnp.logical_not(has_prev))
    def _():
        ext[0] = jnp.zeros((shard, width), BF16)

    @pl.when(jnp.logical_not(has_next))
    def _():
        ext[3] = jnp.zeros((shard, width), BF16)

    group_start = row * (2 * shard)
    send_row = send_ref[...] - (group_start - shard)
    recv_row = recv_ref[...] - group_start
    eight = lax.broadcasted_iota(jnp.int32, (8, edges), 0)
    both = jnp.where(eight == 0, jnp.broadcast_to(send_row, (8, edges)), jnp.broadcast_to(recv_row, (8, edges)))
    cols[...] = jnp.transpose(both)
    count = count_ref[0]

    def rows_of(c):
        return pl.ds(pl.multiple_of(c * chunk, chunk), chunk)

    def live_of(c):
        slots = lax.broadcasted_iota(jnp.int32, (chunk, 1), 0) + c * chunk
        return (slots < count).astype(F32)

    def row_table(index, n):
        return (lax.broadcasted_iota(jnp.int32, (n, chunk), 0) == index).astype(BF16)

    def col_table(index, n):
        return (lax.broadcasted_iota(jnp.int32, (chunk, n), 1) == index).astype(BF16)

    def edge_part(c, carry):
        at = rows_of(c)
        pre_s[at, :] = mm(ef_ref[at, :], wei_ref[:width, :])
        return carry

    lax.fori_loop(0, n_chunks, edge_part, 0)
    psum[...] = jnp.zeros_like(psum)

    to_sib.wait()

    @pl.when(goes)
    def _():
        for r in range(2):
            halo_copy(r).wait_send()

    @pl.when(has_prev)
    def _():
        remote(nf_ref, ext.at[0], 1, (row, sib), there=3).wait_recv()

    @pl.when(has_next)
    def _():
        remote(nf_ref, ext.at[3], 1, (row, sib), there=4).wait_recv()

    latents = ext[...].reshape((4 * shard, width))
    group = latents[shard : 3 * shard]
    table[: 4 * shard, :] = mm(latents, wei_ref[width : 2 * width, :]).astype(BF16)
    table[4 * shard :, :] = mm(group, wei_ref[2 * width :, :]).astype(BF16)
    gain_e = ge_ref[...]

    def forward(c, carry):
        at = rows_of(c)
        s_col, r_col = cols[at, 0:1], cols[at, 1:2]
        pre = (
            pre_s[at, :]
            + mm(col_table(s_col, 4 * shard), table[: 4 * shard, :])
            + mm(col_table(r_col, 2 * shard), table[4 * shard :, :])
        )
        pre_s[at, :] = pre
        act = (pre * sigmoid(pre)).astype(BF16)
        act_s[at, :] = act
        norm, scale = layer_norm(mm(act, weo_ref[...]))
        norm_s[at, :] = norm
        scale_s[at, :] = scale
        message = live_of(c) * norm * gain_e
        edges_out[at, :] = (ef_ref[at, :].astype(F32) + message).astype(BF16)
        r_row = recv_ref[:, at] - group_start
        sums = mm(row_table(r_row, 2 * shard), message.astype(BF16))
        psum[...] += sums.reshape((2, shard, width))
        return carry

    lax.fori_loop(0, n_chunks, forward, 0)

    agg_copy = remote(psum.at[sib], psum_in, 5, (row, sib))
    agg_copy.start()
    nf = nf_ref[...]
    half_pre = mm(nf, wni_ref[:width, :])
    s_sum[...] = jnp.zeros_like(s_sum)
    r_sum[...] = jnp.zeros_like(r_sum)
    dwe[...] = jnp.zeros_like(dwe)
    dwo[...] = jnp.zeros_like(dwo)
    agg_copy.wait()
    agg = (psum[rep] + psum_in[...]).astype(BF16)
    node_pre = half_pre + mm(agg, wni_ref[width:, :])
    node_sig = sigmoid(node_pre)
    node_act = (node_pre * node_sig).astype(BF16)
    node_norm, node_scale = layer_norm(mm(node_act, wno_ref[...]))
    gain_n = gn_ref[...]
    grad = dn_ref[...].astype(F32)
    d_mix = norm_back(grad * gain_n, node_norm, node_scale).astype(BF16)
    slope = node_sig * (1.0 + node_pre * (1.0 - node_sig))
    d_pre_n = (times_transpose(d_mix, wno_ref[...]) * slope).astype(BF16)
    grp_grad[rep] = times_transpose(d_pre_n, wni_ref[width:, :]).astype(BF16)
    grad_copy = remote(grp_grad.at[rep], grp_grad.at[rep], 6, (row, sib))
    grad_copy.start()
    big_n[:width, :] = contract_rows(nf, d_pre_n)
    big_n[width : 2 * width, :] = contract_rows(agg, d_pre_n)
    big_n[2 * width : 3 * width, :] = contract_rows(node_act, d_mix)
    if big_n.shape[0] > 3 * width:
        big_n[3 * width :, :] = jnp.zeros((big_n.shape[0] - 3 * width, width), F32)
    red_n.put(big_n, 0)
    red_n.start_rep()
    nodes_out[...] = (nf.astype(F32) + node_norm * gain_n).astype(BF16)
    gains[0, 1:2, :] = jnp.sum(grad * node_norm, axis=0, keepdims=True)
    gains[0, 0:1, :] = jnp.zeros((1, width), F32)
    direct = grad + times_transpose(d_pre_n, wni_ref[:width, :])
    grad_copy.wait()

    def backward(c, carry):
        at = rows_of(c)
        group_grad = grp_grad[...].reshape((2 * shard, width))
        d_out = de_ref[at, :].astype(F32)
        d_msg = live_of(c) * (d_out + mm(col_table(cols[at, 1:2], 2 * shard), group_grad))
        norm = norm_s[at, :]
        gains[0, 0:1, :] += jnp.sum(d_msg * norm, axis=0, keepdims=True)
        d_mix_e = norm_back(d_msg * gain_e, norm, scale_s[at, :]).astype(BF16)
        dwo[...] += contract_rows(act_s[at, :], d_mix_e)
        pre = pre_s[at, :]
        sig = sigmoid(pre)
        d_pre = (
            times_transpose(d_mix_e, weo_ref[...]) * (sig * (1.0 + pre * (1.0 - sig)))
        ).astype(BF16)
        dwe[...] += contract_rows(ef_ref[at, :], d_pre)
        s_row = send_ref[:, at] - (group_start - shard)
        r_row = recv_ref[:, at] - group_start
        s_sum[...] += mm(row_table(s_row, 4 * shard), d_pre)
        r_sum[...] += mm(row_table(r_row, 2 * shard), d_pre)
        d_edges[at, :] = (d_out + times_transpose(d_pre, wei_ref[:width, :])).astype(BF16)
        return carry

    half = (n_chunks + 1) // 2
    lax.fori_loop(0, half, backward, 0)
    red_n.add_rep()
    red_n.start_level(0)
    lax.fori_loop(half, n_chunks, backward, 0)

    sends_b = s_sum[...].astype(BF16)
    recvs_b = r_sum[...].astype(BF16)
    latents = ext[...].reshape((4 * shard, width))
    big_e[:width, :] = dwe[...]
    big_e[width : 2 * width, :] = contract_rows(latents, sends_b)
    big_e[2 * width : 3 * width, :] = contract_rows(latents[shard : 3 * shard], recvs_b)
    big_e[3 * width : 4 * width, :] = dwo[...]
    if big_e.shape[0] > 4 * width:
        big_e[4 * width :, :] = jnp.zeros((big_e.shape[0] - 4 * width, width), F32)
    red_e.put(big_e, 0)
    red_e.start_rep()

    slot = [0]

    def gain_start(devices):
        out = []
        stage = gain_start.stage
        for device in devices:
            c = pltpu.make_async_remote_copy(
                src_ref=gains.at[stage], dst_ref=gains_in.at[slot[0]],
                send_sem=gsend.at[slot[0]], recv_sem=grecv.at[slot[0]],
                device_id=device, device_id_type=MESH,
            )
            c.start()
            out.append((c, slot[0]))
            slot[0] += 1
        return out

    gain_start.stage = 0

    def gain_add(copies):
        for c, _ in copies:
            c.wait()
        stage = gain_start.stage
        gains[stage + 1] = tree([gains[stage]] + [gains_in[s] for _, s in copies])
        gain_start.stage += 1

    going = gain_start([(row, sib)])

    sender = times_transpose(sends_b, wei_ref[width : 2 * width, :])
    receiver = times_transpose(recvs_b, wei_ref[2 * width :, :])
    halo_out[0] = sender[:shard].astype(BF16)
    halo_out[1] = sender[3 * shard :].astype(BF16)

    def to_prev():
        return remote(halo_out.at[0], halo_in.at[rep], 7, (row - 1, 1), there=9 + rep)

    def to_next():
        return remote(halo_out.at[1], halo_in.at[rep], 8, (row + 1, 0), there=9 + rep)

    @pl.when(has_prev)
    def _():
        to_prev().start()

    @pl.when(has_next)
    def _():
        to_next().start()

    inner = sender[shard : 3 * shard] + receiver
    sib_out[...] = inner.reshape((2, shard, width))
    sib_copy = remote(sib_out.at[sib], sib_in, 11, (row, sib))
    sib_copy.start()

    red_n.add_level(0)
    for level in range(1, levels):
        red_n.start_level(level)
        if level == 1:
            red_e.add_rep()
            gain_add(going)
            red_e.start_level(0)
            going = gain_start([(red_e.partner(0, k)[0], rep) for k in range(1, digits[0][1])])
        red_n.add_level(level)
    red_n.start_gather(levels - 1)

    sib_copy.wait()
    total = direct + sib_out[rep] + sib_in[...]

    @pl.when(has_prev)
    def _():
        to_prev().wait_send()

    @pl.when(has_next)
    def _():
        to_next().wait_send()

    hears = ((rep == 0) & has_prev) | ((rep == 1) & has_next)

    @pl.when(hears)
    def _():
        for r in range(2):
            remote(halo_out.at[0], halo_in.at[r], 7, (row, sib), there=9 + r).wait_recv()
        d_nodes[...] = (total + (halo_in[0].astype(F32) + halo_in[1].astype(F32))).astype(BF16)

    @pl.when(jnp.logical_not(hears))
    def _():
        d_nodes[...] = total.astype(BF16)

    if levels == 1:
        red_e.add_rep()
        gain_add(going)
        red_e.start_level(0)
        going = gain_start([(red_e.partner(0, k)[0], rep) for k in range(1, digits[0][1])])
    red_n.wait()
    if levels > 1:
        red_n.start_gather(levels - 2)
    for level in range(levels):
        red_e.add_level(level)
        gain_add(going)
        if level + 1 < levels:
            red_e.start_level(level + 1)
            going = gain_start(
                [(red_e.partner(level + 1, k)[0], rep) for k in range(1, digits[level + 1][1])]
            )
    for level in reversed(range(levels)):
        red_e.start_gather(level)
        if level < levels - 1:
            red_n.wait()
            if level > 0:
                red_n.start_gather(level - 1)
            else:
                red_n.start_gather_rep()
        red_e.wait()
    if levels == 1:
        red_n.start_gather_rep()
    red_e.start_gather_rep()
    o_ge[...] = gains[levels + 1, 0:1, :]
    o_gn[...] = gains[levels + 1, 1:2, :]
    red_n.wait()
    for h in range(2):
        lanes = slice(h * LANES, (h + 1) * LANES)
        full = red_n.take(h)
        o_wni[:, lanes] = full[: 2 * width]
        o_wno[:, lanes] = full[2 * width : 3 * width]
    red_e.wait()
    for h in range(2):
        lanes = slice(h * LANES, (h + 1) * LANES)
        full = red_e.take(h)
        o_wei[:, lanes] = full[: 3 * width]
        o_weo[:, lanes] = full[3 * width : 4 * width]


def local(
    n_row,
    node_feats, edge_feats, senders, receivers, edge_count,
    w_edge_in, w_edge_out, gain_edge, w_node_in, w_node_out, gain_node,
    d_nodes_out, d_edges_out,
):
    shard, width = node_feats.shape
    edges = edge_feats.shape[0]
    chunk = min(edges, 256)
    digits = digits_of(n_row)
    radices = tuple(r for _, r in digits)
    partners = sum(r - 1 for r in radices)
    vmem, smem = pl.BlockSpec(memory_space=pltpu.VMEM), pl.BlockSpec(memory_space=pltpu.SMEM)

    def reduction(rows):
        block = -(-rows // (16 * n_row)) * 16
        tail = (block, LANES)
        levels = [
            pltpu.VMEM((r - 1,) + radices[i + 1 :] + tail, BF16) for i, r in enumerate(radices)
        ]
        return (
            block * n_row,
            [pltpu.VMEM((2,) + radices + tail, BF16), pltpu.VMEM(radices + tail, BF16),
             pltpu.VMEM((2,) + radices + tail, BF16)],
            levels,
        )

    rows_n, bufs_n, levels_n = reduction(3 * width)
    rows_e, bufs_e, levels_e = reduction(4 * width)
    copies = 2 * (1 + partners)
    dma = pltpu.SemaphoreType.DMA
    scratch = [
        pltpu.VMEM((4, shard, width), BF16),
        pltpu.VMEM((6 * shard, width), BF16),
        pltpu.VMEM((edges, 8), jnp.int32),
        pltpu.VMEM((edges, width), F32),
        pltpu.VMEM((edges, width), F32),
        pltpu.VMEM((edges, 1), F32),
        pltpu.VMEM((edges, width), BF16),
        pltpu.VMEM((2, shard, width), F32),
        pltpu.VMEM((shard, width), F32),
        pltpu.VMEM((2, shard, width), BF16),
        pltpu.VMEM((4 * shard, width), F32),
        pltpu.VMEM((2 * shard, width), F32),
        pltpu.VMEM((width, width), F32),
        pltpu.VMEM((width, width), F32),
        pltpu.VMEM((rows_e, width), F32),
        pltpu.VMEM((rows_n, width), F32),
        pltpu.VMEM((2, shard, width), BF16),
        pltpu.VMEM((2, shard, width), BF16),
        pltpu.VMEM((2, shard, width), F32),
        pltpu.VMEM((shard, width), F32),
        pltpu.VMEM((len(digits) + 2, 8, width), F32),
        pltpu.VMEM((1 + partners, 8, width), F32),
        *bufs_n,
        *bufs_e,
        dma((12,)), dma((12,)),
        dma((copies,)), dma((copies,)), dma((copies,)), dma((copies,)),
        dma((1 + partners,)), dma((1 + partners,)),
        *levels_n,
        *levels_e,
    ]
    out = pl.pallas_call(
        functools.partial(kernel, digits, n_row, chunk),
        out_shape=(
            jax.ShapeDtypeStruct((shard, width), BF16),
            jax.ShapeDtypeStruct((edges, width), BF16),
            jax.ShapeDtypeStruct((shard, width), BF16),
            jax.ShapeDtypeStruct((edges, width), BF16),
            jax.ShapeDtypeStruct(w_edge_in.shape, BF16),
            jax.ShapeDtypeStruct(w_edge_out.shape, BF16),
            jax.ShapeDtypeStruct((1, width), F32),
            jax.ShapeDtypeStruct(w_node_in.shape, BF16),
            jax.ShapeDtypeStruct(w_node_out.shape, BF16),
            jax.ShapeDtypeStruct((1, width), F32),
        ),
        in_specs=[vmem] * 4 + [smem] + [vmem] * 8,
        out_specs=tuple([vmem] * 10),
        scratch_shapes=scratch,
        compiler_params=pltpu.CompilerParams(
            collective_id=0, has_side_effects=True, vmem_limit_bytes=60 * 2**20
        ),
        name="layer",
    )(
        node_feats, edge_feats, senders[None, :], receivers[None, :], edge_count,
        w_edge_in, w_edge_out, gain_edge[None, :], w_node_in, w_node_out, gain_node[None, :],
        d_nodes_out, d_edges_out,
    )
    return (*out[:6], out[6][0], *out[7:9], out[9][0])


def padded(x, sides, width):
    for axis, dim in sides:
        devices, length = (lax.axis_size(axis), x.shape[dim])
        up = [(i, (i + 1) % devices) for i in range(devices - 1)]
        down = [(j, i) for i, j in up]
        last = lax.slice_in_dim(x, length - width, length, axis=dim)
        first = lax.slice_in_dim(x, 0, width, axis=dim)
        before = lax.ppermute(last, axis, up)
        after = lax.ppermute(first, axis, down)
        x = jnp.concatenate([before, x, after], axis=dim)
    return x


def from_behind(value, axis, steps):
    count = lax.axis_size(axis)
    first, last = (max(0, -steps), min(count, count - steps))
    return lax.ppermute(value, axis, [(source, source + steps) for source in range(first, last)])


def plain_slope(pre):
    sigmoid = jax.nn.sigmoid(pre)
    return sigmoid * (1.0 + pre * (1.0 - sigmoid))


def plain_norm(values):
    centred = values - jnp.mean(values, axis=-1, keepdims=True)
    inv_scale = lax.rsqrt(jnp.mean(centred * centred, axis=-1, keepdims=True) + 1e-05)
    return (centred * inv_scale, inv_scale)


def plain_back(upstream, normed, inv_scale):
    return inv_scale * (
        upstream
        - jnp.mean(upstream, axis=-1, keepdims=True)
        - normed * jnp.mean(upstream * normed, axis=-1, keepdims=True)
    )


def plain_rows(left, right):
    return lax.dot_general(
        left, right, (((0,), (0,)), ((), ())), preferred_element_type=jnp.float32
    )


def plain_times(left, right):
    return lax.dot_general(
        left, right, (((1,), (1,)), ((), ())), preferred_element_type=jnp.float32
    )


def plain(
    node_feats,
    edge_feats,
    senders,
    receivers,
    edge_count,
    w_edge_in,
    w_edge_out,
    gain_edge,
    w_node_in,
    w_node_out,
    gain_node,
    d_nodes_out,
    d_edges_out,
):
    width = node_feats.shape[1]
    edge_rows = edge_feats.shape[0]
    grouped = lax.all_gather(node_feats, "rep", axis=0, tiled=True)
    group_rows = grouped.shape[0]
    rim_rows = group_rows // 2
    extended = padded(grouped, (("row", 0),), rim_rows)
    group_start = lax.axis_index("row") * group_rows
    recv_local = receivers - group_start
    send_local = senders - group_start + rim_rows
    slots = jnp.arange(edge_rows, dtype=jnp.int32)
    live_mask = (slots < edge_count[0]).astype(jnp.float32)[:, None]
    edge_input = jnp.concatenate(
        [edge_feats, jnp.take(extended, send_local, axis=0), jnp.take(grouped, recv_local, axis=0)],
        axis=1,
    )
    edge_pre = jnp.dot(edge_input, w_edge_in, preferred_element_type=jnp.float32)
    edge_act = jax.nn.silu(edge_pre).astype(jnp.bfloat16)
    edge_mix = jnp.dot(edge_act, w_edge_out, preferred_element_type=jnp.float32)
    edge_norm, edge_scale = plain_norm(edge_mix)
    message = live_mask * edge_norm * gain_edge
    edges_out = (edge_feats.astype(jnp.float32) + message).astype(jnp.bfloat16)
    message_b = message.astype(jnp.bfloat16)
    recv_table = (
        lax.broadcasted_iota(jnp.int32, (group_rows, edge_rows), 0) == recv_local[None, :]
    ).astype(jnp.bfloat16)
    partial_sums = jnp.dot(recv_table, message_b, preferred_element_type=jnp.float32)
    aggregate = lax.psum_scatter(partial_sums, "rep", scatter_dimension=0, tiled=True)
    node_input = jnp.concatenate([node_feats, aggregate.astype(jnp.bfloat16)], axis=1)
    node_pre = jnp.dot(node_input, w_node_in, preferred_element_type=jnp.float32)
    node_act = jax.nn.silu(node_pre).astype(jnp.bfloat16)
    node_mix = jnp.dot(node_act, w_node_out, preferred_element_type=jnp.float32)
    node_norm, node_scale = plain_norm(node_mix)
    nodes_out = (node_feats.astype(jnp.float32) + node_norm * gain_node).astype(jnp.bfloat16)
    grad_nodes = d_nodes_out.astype(jnp.float32)
    d_gain_node = jnp.sum(grad_nodes * node_norm, axis=0)
    d_node_mix = plain_back(grad_nodes * gain_node, node_norm, node_scale).astype(jnp.bfloat16)
    d_w_node_out = plain_rows(node_act, d_node_mix)
    d_node_pre = (plain_times(d_node_mix, w_node_out) * plain_slope(node_pre)).astype(
        jnp.bfloat16
    )
    d_w_node_in = plain_rows(node_input, d_node_pre)
    d_node_input = plain_times(d_node_pre, w_node_in)
    d_aggregate = d_node_input[:, width:].astype(jnp.bfloat16)
    d_direct = grad_nodes + d_node_input[:, :width]
    group_grad = lax.all_gather(d_aggregate, "rep", axis=0, tiled=True)
    d_message = live_mask * (
        d_edges_out.astype(jnp.float32)
        + jnp.take(group_grad, recv_local, axis=0).astype(jnp.float32)
    )
    d_gain_edge = jnp.sum(d_message * edge_norm, axis=0)
    d_edge_mix = plain_back(d_message * gain_edge, edge_norm, edge_scale).astype(jnp.bfloat16)
    d_w_edge_out = plain_rows(edge_act, d_edge_mix)
    d_edge_pre = (plain_times(d_edge_mix, w_edge_out) * plain_slope(edge_pre)).astype(
        jnp.bfloat16
    )
    d_w_edge_in = plain_rows(edge_input, d_edge_pre)
    d_edge_input = plain_times(d_edge_pre, w_edge_in)
    d_edges = (d_edges_out.astype(jnp.float32) + d_edge_input[:, :width]).astype(jnp.bfloat16)
    d_sender = d_edge_input[:, width : 2 * width].astype(jnp.bfloat16)
    d_receiver = d_edge_input[:, 2 * width :].astype(jnp.bfloat16)
    send_table = (
        lax.broadcasted_iota(jnp.int32, (group_rows + 2 * rim_rows, edge_rows), 0)
        == send_local[None, :]
    ).astype(jnp.bfloat16)
    send_sums = jnp.dot(send_table, d_sender, preferred_element_type=jnp.float32)
    recv_sums = jnp.dot(recv_table, d_receiver, preferred_element_type=jnp.float32)
    from_next = from_behind(send_sums[:rim_rows].astype(jnp.bfloat16), "row", -1).astype(
        jnp.float32
    )
    from_prev = from_behind(
        send_sums[group_rows + rim_rows :].astype(jnp.bfloat16), "row", 1
    ).astype(jnp.float32)
    inner = send_sums[rim_rows : rim_rows + group_rows]
    inner = jnp.concatenate([inner[:rim_rows] + from_prev, inner[rim_rows:] + from_next], axis=0)
    edge_terms = lax.psum_scatter(
        inner.astype(jnp.bfloat16), "rep", scatter_dimension=0, tiled=True
    ).astype(jnp.float32) + lax.psum_scatter(
        recv_sums.astype(jnp.bfloat16), "rep", scatter_dimension=0, tiled=True
    ).astype(
        jnp.float32
    )
    d_nodes = (d_direct + edge_terms).astype(jnp.bfloat16)
    summed = lax.psum(
        (d_w_edge_in, d_w_edge_out, d_gain_edge, d_w_node_in, d_w_node_out, d_gain_node),
        ("row", "rep"),
    )
    return (
        nodes_out,
        edges_out,
        d_nodes,
        d_edges,
        summed[0].astype(jnp.bfloat16),
        summed[1].astype(jnp.bfloat16),
        summed[2],
        summed[3].astype(jnp.bfloat16),
        summed[4].astype(jnp.bfloat16),
        summed[5],
    )


def solution(mesh):
    split, flat, whole = P(("row", "rep"), None), P(("row", "rep")), P()
    layer = functools.partial(local, mesh.shape["row"]) if mesh.shape["rep"] == 2 else plain
    return jax.shard_map(
        layer,
        mesh=mesh,
        in_specs=(split, split, flat, flat, flat) + (whole,) * 6 + (split, split),
        out_specs=(split,) * 4 + (whole,) * 6,
        check_vma=False,
    )
```

```python
import functools

import jax
import jax.numpy as jnp
from jax import lax
from jax.experimental import pallas as pl
from jax.experimental.pallas import tpu as pltpu
from jax.sharding import PartitionSpec as P

F32 = jnp.float32
BF16 = jnp.bfloat16
LANES = 128
MESH = pl.DeviceIdType.MESH


def mm(left, right):
    return jnp.dot(left, right, preferred_element_type=F32)


def contract_rows(left, right):
    return lax.dot_general(left, right, (((0,), (0,)), ((), ())), preferred_element_type=F32)


def times_transpose(left, right):
    return lax.dot_general(left, right, (((1,), (1,)), ((), ())), preferred_element_type=F32)


def sigmoid(v):
    return 1.0 / (1.0 + jnp.exp(-v))


def layer_norm(values):
    centred = values - jnp.mean(values, axis=-1, keepdims=True)
    inv_scale = lax.rsqrt(jnp.mean(centred * centred, axis=-1, keepdims=True) + 1e-05)
    return (centred * inv_scale, inv_scale)


def norm_back(upstream, normed, inv_scale):
    return inv_scale * (
        upstream
        - jnp.mean(upstream, axis=-1, keepdims=True)
        - normed * jnp.mean(upstream * normed, axis=-1, keepdims=True)
    )


def digits_of(n_row):
    out, stride = [], 1
    while stride < n_row:
        radix = 4 if n_row % (stride * 4) == 0 else 2
        out.append((stride, radix))
        stride *= radix
    return out


def tree(values):
    while len(values) > 1:
        values = [values[i] + values[i + 1] for i in range(0, len(values), 2)]
    return values[0]


class Reduction:
    def __init__(self, rank, digits, buf, recv_rep, recvs, gathered, sends, sems):
        self.row, self.rep, self.digits = rank[0], rank[1], digits
        self.buf, self.recv_rep, self.recvs, self.gathered = buf, recv_rep, recvs, gathered
        self.send, self.recv = sends, sems
        self.mine = [(self.row // s) % r for s, r in digits]
        self.live = []
        self.slot = 0

    def partner(self, level, k):
        stride, _ = self.digits[level]
        d = self.mine[level]
        other = jnp.bitwise_xor(d, k)
        return self.row + (other - d) * stride, other

    def copy(self, src, dst, device):
        c = pltpu.make_async_remote_copy(
            src_ref=src,
            dst_ref=dst,
            send_sem=self.send.at[self.slot],
            recv_sem=self.recv.at[self.slot],
            device_id=device,
            device_id_type=MESH,
        )
        self.slot += 1
        c.start()
        self.live.append(c)

    def wait(self):
        for c in self.live:
            c.wait()
        self.live = []

    def start_rep(self):
        d, radix = self.mine[0], self.digits[0][1]
        for k in [*range(1, radix), 0]:
            block = jnp.bitwise_xor(d, k)
            self.copy(self.buf.at[1 - self.rep, block], self.recv_rep.at[block], (self.row, 1 - self.rep))

    def at(self, ref, level):
        for d in self.mine[:level]:
            ref = ref.at[d]
        return ref

    def add_rep(self):
        arriving, self.live = self.live, []
        d, radix = self.mine[0], self.digits[0][1]
        for c, k in zip(arriving, [*range(1, radix), 0]):
            c.wait()
            block = jnp.bitwise_xor(d, k)
            mine = self.buf.at[self.rep, block]
            mine[...] = (mine[...].astype(F32) + self.recv_rep[block].astype(F32)).astype(BF16)
            if k:
                self.copy(mine, self.recvs[0].at[k - 1], (self.partner(0, k)[0], self.rep))

    def start_level(self, level):
        ref = self.at(self.buf.at[self.rep], level)
        for k in range(1, self.digits[level][1]):
            row, other = self.partner(level, k)
            self.copy(ref.at[other], self.recvs[level].at[k - 1], (row, self.rep))

    def add_level(self, level):
        self.wait()
        ref = self.at(self.buf.at[self.rep], level + 1)
        parts = [ref[...].astype(F32)]
        parts += [self.recvs[level][k].astype(F32) for k in range(self.digits[level][1] - 1)]
        total = tree(parts).astype(BF16)
        if level + 1 == len(self.digits):
            self.at(self.gathered.at[self.rep], level + 1)[...] = total
        else:
            ref[...] = total

    def start_gather(self, level):
        ref = self.at(self.gathered.at[self.rep], level + 1)
        for k in range(1, self.digits[level][1]):
            row, _ = self.partner(level, k)
            self.copy(ref, ref, (row, self.rep))

    def start_gather_last(self):
        self.start_gather(0)
        ref = self.gathered.at[self.rep, self.mine[0]]
        self.copy(ref, ref, (self.row, 1 - self.rep))

    def forward(self):
        radix = self.digits[0][1]
        arriving, self.live = self.live[: radix - 1], self.live[radix - 1 :]
        for c, k in zip(arriving, range(1, radix)):
            c.wait()
            ref = self.gathered.at[self.rep, jnp.bitwise_xor(self.mine[0], k)]
            self.copy(ref, ref, (self.row, 1 - self.rep))

    def put(self, array):
        for h in range(2):
            part = array[:, h * LANES : (h + 1) * LANES].astype(BF16)
            self.buf[h] = part.reshape(self.buf.shape[1:])


def kernel(
    digits,
    n_row,
    chunk,
    h_nf, h_ef, h_send, h_recv, count_ref,
    h_wei, h_weo, h_ge, h_wni, h_wno, h_gn, h_dn, h_de,
    nodes_out, edges_out, d_nodes, d_edges, gat_e, gat_n, o_gains,
    nf_ref, ef_ref, send_ref, recv_ref,
    wei_ref, weo_ref, ge_ref, wni_ref, wno_ref, gn_ref, dn_ref, de_ref, load_sem,
    ext, table, cols, pre_s, norm_s, scale_s, act_s, psum, psum_in, grp_grad,
    s_sum, r_sum, dwe, dwo, big_e, big_n, halo_out, halo_in, sib_out, sib_in,
    gains, gains_in,
    d_pre_s, buf_n, rep_n, buf_e, rep_e,
    send_sem, recv_sem, nsend, nrecv, esend, erecv, gsend, grecv,
    *level_refs,
):
    row, rep = lax.axis_index("row"), lax.axis_index("rep")
    sib = 1 - rep
    shard, width = nf_ref.shape
    edges = ef_ref.shape[0]
    n_chunks = edges // chunk
    levels = len(digits)
    has_prev, has_next = row > 0, row < n_row - 1
    red_n = Reduction((row, rep), digits, buf_n, rep_n, level_refs[:levels], gat_n, nsend, nrecv)
    red_e = Reduction((row, rep), digits, buf_e, rep_e, level_refs[levels:], gat_e, esend, erecv)

    def remote(src, dst, slot, device, there=None):
        return pltpu.make_async_remote_copy(
            src_ref=src, dst_ref=dst, send_sem=send_sem.at[slot],
            recv_sem=recv_sem.at[slot if there is None else there],
            device_id=device, device_id_type=MESH,
        )

    pairs = (
        (h_ef, ef_ref), (h_wei, wei_ref), (h_nf, nf_ref), (h_send, send_ref), (h_recv, recv_ref),
        (h_weo, weo_ref), (h_ge, ge_ref), (h_wni, wni_ref), (h_wno, wno_ref), (h_gn, gn_ref),
        (h_dn, dn_ref), (h_de, de_ref),
    )
    loads = [pltpu.make_async_copy(a, b, load_sem.at[i]) for i, (a, b) in enumerate(pairs)]
    for load in loads:
        load.start()

    barrier = pltpu.get_barrier_semaphore()

    def greet(device):
        pl.semaphore_signal(barrier, inc=1, device_id=device, device_id_type=MESH)

    greet((row, sib))
    level_partners = 0
    for level, (_, radix) in enumerate(digits):
        for k in range(1, radix):
            greet((red_n.partner(level, k)[0], rep))
            level_partners += 1

    @pl.when(has_prev)
    def _():
        for r in range(2):
            greet((row - 1, r))

    @pl.when(has_next)
    def _():
        for r in range(2):
            greet((row + 1, r))

    around = 2 * (jnp.int32(has_prev) + jnp.int32(has_next))
    pl.semaphore_wait(barrier, 1 + level_partners + around)

    own = 1 + rep
    to_sib = remote(h_nf, ext.at[own], 0, (row, sib))
    to_sib.start()
    goes = ((rep == 0) & has_prev) | ((rep == 1) & has_next)
    target = jnp.where(rep == 0, row - 1, row + 1)
    place = jnp.where(rep == 0, 3, 0)

    def halo_copy(r):
        return remote(h_nf, ext.at[place], 1 + r, (target, r), there=jnp.where(rep == 0, 4, 3))

    @pl.when(goes)
    def _():
        for r in range(2):
            halo_copy(r).start()

    for load in loads[:5]:
        load.wait()
    ext[own] = nf_ref[...]

    @pl.when(jnp.logical_not(has_prev))
    def _():
        ext[0] = jnp.zeros((shard, width), BF16)

    @pl.when(jnp.logical_not(has_next))
    def _():
        ext[3] = jnp.zeros((shard, width), BF16)

    group_start = row * (2 * shard)
    send_row = send_ref[...] - (group_start - shard)
    recv_row = recv_ref[...] - group_start
    eight = lax.broadcasted_iota(jnp.int32, (8, edges), 0)
    both = jnp.where(eight == 0, jnp.broadcast_to(send_row, (8, edges)), jnp.broadcast_to(recv_row, (8, edges)))
    cols[...] = jnp.transpose(both)
    count = count_ref[0]

    def rows_of(c):
        return pl.ds(pl.multiple_of(c * chunk, chunk), chunk)

    def live_of(c):
        slots = lax.broadcasted_iota(jnp.int32, (chunk, 1), 0) + c * chunk
        return (slots < count).astype(F32)

    def row_table(index, n):
        return (lax.broadcasted_iota(jnp.int32, (n, chunk), 0) == index).astype(BF16)

    def col_table(index, n):
        return (lax.broadcasted_iota(jnp.int32, (chunk, n), 1) == index).astype(BF16)

    def edge_part(c, carry):
        at = rows_of(c)
        pre_s[at, :] = mm(ef_ref[at, :], wei_ref[:width, :])
        return carry

    lax.fori_loop(0, n_chunks, edge_part, 0)
    psum[...] = jnp.zeros_like(psum)
    for load in loads[5:]:
        load.wait()

    to_sib.wait()

    @pl.when(goes)
    def _():
        for r in range(2):
            halo_copy(r).wait_send()

    @pl.when(has_prev)
    def _():
        remote(nf_ref, ext.at[0], 1, (row, sib), there=3).wait_recv()

    @pl.when(has_next)
    def _():
        remote(nf_ref, ext.at[3], 1, (row, sib), there=4).wait_recv()

    latents = ext[...].reshape((4 * shard, width))
    group = latents[shard : 3 * shard]
    table[: 4 * shard, :] = mm(latents, wei_ref[width : 2 * width, :]).astype(BF16)
    table[4 * shard :, :] = mm(group, wei_ref[2 * width :, :]).astype(BF16)
    gain_e = ge_ref[...]

    def forward(c, carry):
        at = rows_of(c)
        s_col, r_col = cols[at, 0:1], cols[at, 1:2]
        pre = (
            pre_s[at, :]
            + mm(col_table(s_col, 4 * shard), table[: 4 * shard, :])
            + mm(col_table(r_col, 2 * shard), table[4 * shard :, :])
        )
        pre_s[at, :] = pre
        act = (pre * sigmoid(pre)).astype(BF16)
        act_s[at, :] = act
        norm, scale = layer_norm(mm(act, weo_ref[...]))
        norm_s[at, :] = norm
        scale_s[at, :] = scale
        message = live_of(c) * norm * gain_e
        r_row = recv_ref[:, at] - group_start
        sums = mm(row_table(r_row, 2 * shard), message.astype(BF16))
        psum[...] += sums.reshape((2, shard, width))
        return carry

    lax.fori_loop(0, n_chunks, forward, 0)

    agg_copy = remote(psum.at[sib], psum_in, 5, (row, sib))
    agg_copy.start()
    nf = nf_ref[...]
    half_pre = mm(nf, wni_ref[:width, :])
    s_sum[...] = jnp.zeros_like(s_sum)
    r_sum[...] = jnp.zeros_like(r_sum)
    dwe[...] = jnp.zeros_like(dwe)
    dwo[...] = jnp.zeros_like(dwo)

    def finish_edges(c, carry):
        at = rows_of(c)
        message = live_of(c) * norm_s[at, :] * gain_e
        edges_out[at, :] = (ef_ref[at, :].astype(F32) + message).astype(BF16)
        return carry

    lax.fori_loop(0, n_chunks, finish_edges, 0)
    agg_copy.wait()
    agg = (psum[rep] + psum_in[...]).astype(BF16)
    node_pre = half_pre + mm(agg, wni_ref[width:, :])
    node_sig = sigmoid(node_pre)
    node_act = (node_pre * node_sig).astype(BF16)
    node_norm, node_scale = layer_norm(mm(node_act, wno_ref[...]))
    gain_n = gn_ref[...]
    grad = dn_ref[...].astype(F32)
    d_mix = norm_back(grad * gain_n, node_norm, node_scale).astype(BF16)
    slope = node_sig * (1.0 + node_pre * (1.0 - node_sig))
    d_pre_n = (times_transpose(d_mix, wno_ref[...]) * slope).astype(BF16)
    grp_grad[rep] = times_transpose(d_pre_n, wni_ref[width:, :]).astype(BF16)
    grad_copy = remote(grp_grad.at[rep], grp_grad.at[rep], 6, (row, sib))
    grad_copy.start()
    big_n[:width, :] = contract_rows(nf, d_pre_n)
    big_n[width : 2 * width, :] = contract_rows(agg, d_pre_n)
    big_n[2 * width : 3 * width, :] = contract_rows(node_act, d_mix)
    if big_n.shape[0] > 3 * width:
        big_n[3 * width :, :] = jnp.zeros((big_n.shape[0] - 3 * width, width), F32)
    red_n.put(big_n)
    red_n.start_rep()
    nodes_out[...] = (nf.astype(F32) + node_norm * gain_n).astype(BF16)
    gains[0, 1:2, :] = jnp.sum(grad * node_norm, axis=0, keepdims=True)
    gains[0, 0:1, :] = jnp.zeros((1, width), F32)
    direct = grad + times_transpose(d_pre_n, wni_ref[:width, :])
    grad_copy.wait()

    def backward(c, carry):
        at = rows_of(c)
        group_grad = grp_grad[...].reshape((2 * shard, width))
        d_out = de_ref[at, :].astype(F32)
        d_msg = live_of(c) * (d_out + mm(col_table(cols[at, 1:2], 2 * shard), group_grad))
        norm = norm_s[at, :]
        gains[0, 0:1, :] += jnp.sum(d_msg * norm, axis=0, keepdims=True)
        d_mix_e = norm_back(d_msg * gain_e, norm, scale_s[at, :]).astype(BF16)
        dwo[...] += contract_rows(act_s[at, :], d_mix_e)
        pre = pre_s[at, :]
        sig = sigmoid(pre)
        d_pre = (
            times_transpose(d_mix_e, weo_ref[...]) * (sig * (1.0 + pre * (1.0 - sig)))
        ).astype(BF16)
        dwe[...] += contract_rows(ef_ref[at, :], d_pre)
        s_row = send_ref[:, at] - (group_start - shard)
        r_row = recv_ref[:, at] - group_start
        s_sum[...] += mm(row_table(s_row, 4 * shard), d_pre)
        r_sum[...] += mm(row_table(r_row, 2 * shard), d_pre)
        d_pre_s[at, :] = d_pre
        return carry

    red_n.add_rep()
    half = (n_chunks + 1) // 2
    lax.fori_loop(0, half, backward, 0)
    lax.fori_loop(half, n_chunks, backward, 0)

    sends_b = s_sum[...].astype(BF16)
    recvs_b = r_sum[...].astype(BF16)
    latents = ext[...].reshape((4 * shard, width))
    big_e[:width, :] = dwe[...]
    big_e[width : 2 * width, :] = contract_rows(latents, sends_b)
    big_e[2 * width : 3 * width, :] = contract_rows(latents[shard : 3 * shard], recvs_b)
    big_e[3 * width : 4 * width, :] = dwo[...]
    if big_e.shape[0] > 4 * width:
        big_e[4 * width :, :] = jnp.zeros((big_e.shape[0] - 4 * width, width), F32)
    red_e.put(big_e)
    red_e.start_rep()

    slot = [0]

    def gain_start(devices):
        out = []
        stage = gain_start.stage
        for device in devices:
            c = pltpu.make_async_remote_copy(
                src_ref=gains.at[stage], dst_ref=gains_in.at[slot[0]],
                send_sem=gsend.at[slot[0]], recv_sem=grecv.at[slot[0]],
                device_id=device, device_id_type=MESH,
            )
            c.start()
            out.append((c, slot[0]))
            slot[0] += 1
        return out

    gain_start.stage = 0

    def gain_add(copies):
        for c, _ in copies:
            c.wait()
        stage = gain_start.stage
        gains[stage + 1] = tree([gains[stage]] + [gains_in[s] for _, s in copies])
        gain_start.stage += 1

    going = gain_start([(row, sib)])

    sender = times_transpose(sends_b, wei_ref[width : 2 * width, :])
    receiver = times_transpose(recvs_b, wei_ref[2 * width :, :])
    halo_out[0] = sender[:shard].astype(BF16)
    halo_out[1] = sender[3 * shard :].astype(BF16)

    def to_prev():
        return remote(halo_out.at[0], halo_in.at[rep], 7, (row - 1, 1), there=9 + rep)

    def to_next():
        return remote(halo_out.at[1], halo_in.at[rep], 8, (row + 1, 0), there=9 + rep)

    @pl.when(has_prev)
    def _():
        to_prev().start()

    @pl.when(has_next)
    def _():
        to_next().start()

    inner = sender[shard : 3 * shard] + receiver
    sib_out[...] = inner.reshape((2, shard, width))
    sib_copy = remote(sib_out.at[sib], sib_in, 11, (row, sib))
    sib_copy.start()

    def stage_of(level):
        return [(red_e.partner(level, k)[0], rep) for k in range(1, digits[level][1])]

    red_n.add_level(0)
    if levels > 1:
        red_n.start_level(1)
    red_e.add_rep()
    gain_add(going)
    going = gain_start(stage_of(0))

    def finish_d_edges(c, carry):
        at = rows_of(c)
        back = times_transpose(d_pre_s[at, :], wei_ref[:width, :])
        d_edges[at, :] = (de_ref[at, :].astype(F32) + back).astype(BF16)
        return carry

    for level in range(1, levels):
        red_n.add_level(level)
        if level + 1 < levels:
            red_n.start_level(level + 1)
    if levels > 1:
        red_n.start_gather(levels - 1)
    lax.fori_loop(0, n_chunks, finish_d_edges, 0)

    sib_copy.wait()
    total = direct + sib_out[rep] + sib_in[...]

    @pl.when(has_prev)
    def _():
        to_prev().wait_send()

    @pl.when(has_next)
    def _():
        to_next().wait_send()

    hears = ((rep == 0) & has_prev) | ((rep == 1) & has_next)

    @pl.when(hears)
    def _():
        for r in range(2):
            remote(halo_out.at[0], halo_in.at[r], 7, (row, sib), there=9 + r).wait_recv()
        d_nodes[...] = (total + (halo_in[0].astype(F32) + halo_in[1].astype(F32))).astype(BF16)

    @pl.when(jnp.logical_not(hears))
    def _():
        d_nodes[...] = total.astype(BF16)

    for level in reversed(range(1, levels)):
        red_n.wait()
        if level > 1:
            red_n.start_gather(level - 1)
    red_n.start_gather_last()
    for level in range(levels):
        red_e.add_level(level)
        if level + 1 < levels:
            red_e.start_level(level + 1)
        elif levels > 1:
            red_e.start_gather(level)
        gain_add(going)
        if level + 1 < levels:
            going = gain_start(stage_of(level + 1))
        if level == 0:
            red_n.forward()
    o_gains[...] = gains[levels + 1]
    for level in reversed(range(1, levels)):
        red_e.wait()
        if level > 1:
            red_e.start_gather(level - 1)
    red_e.start_gather_last()
    red_n.wait()
    red_e.forward()
    red_e.wait()


def unpack(*refs):
    ins, outs, held, load_sem, store_sem = refs[:7], refs[7:17], refs[17:24], refs[24], refs[25]
    loads = [pltpu.make_async_copy(a, b, load_sem.at[i]) for i, (a, b) in enumerate(zip(ins, held))]
    for load in loads:
        load.start()
    stores = [pltpu.make_async_copy(held[i], outs[i], store_sem.at[i]) for i in range(4)]
    for load, store in zip(loads, stores):
        load.wait()
        store.start()
    for load in loads[4:]:
        load.wait()
    gat_e, gat_n, gains = held[4:]
    o_wei, o_weo, o_ge, o_wni, o_wno, o_gn = outs[4:]
    o_ge[...] = gains[0:1, :]
    o_gn[...] = gains[1:2, :]
    for h in range(2):
        lanes = slice(h * LANES, (h + 1) * LANES)
        full = gat_e[h].reshape((-1, LANES))
        o_wei[:, lanes] = full[: o_wei.shape[0]]
        o_weo[:, lanes] = full[o_wei.shape[0] : o_wei.shape[0] + o_weo.shape[0]]
        full = gat_n[h].reshape((-1, LANES))
        o_wni[:, lanes] = full[: o_wni.shape[0]]
        o_wno[:, lanes] = full[o_wni.shape[0] : o_wni.shape[0] + o_wno.shape[0]]
    for store in stores:
        store.wait()


def local(
    n_row,
    node_feats, edge_feats, senders, receivers, edge_count,
    w_edge_in, w_edge_out, gain_edge, w_node_in, w_node_out, gain_node,
    d_nodes_out, d_edges_out,
):
    shard, width = node_feats.shape
    edges = edge_feats.shape[0]
    chunk = min(edges, 512)
    digits = digits_of(n_row)
    radices = tuple(r for _, r in digits)
    partners = sum(r - 1 for r in radices)
    hbm = pl.BlockSpec(memory_space=pl.ANY)
    vmem, smem = pl.BlockSpec(memory_space=pltpu.VMEM), pl.BlockSpec(memory_space=pltpu.SMEM)

    def reduction(rows, radices):
        block = -(-rows // (16 * n_row)) * 16
        tail = (block, LANES)
        levels = [
            pltpu.VMEM((r - 1,) + radices[i + 1 :] + tail, BF16) for i, r in enumerate(radices)
        ]
        return (
            block * n_row,
            [pltpu.VMEM((2,) + radices + tail, BF16), pltpu.VMEM(radices + tail, BF16)],
            levels,
            jax.ShapeDtypeStruct((2,) + radices + tail, BF16),
        )

    rows_n, bufs_n, levels_n, gathered_n = reduction(3 * width, radices)
    rows_e, bufs_e, levels_e, gathered_e = reduction(4 * width, radices)
    copies = 2 * (max(radices) + partners)
    dma = pltpu.SemaphoreType.DMA
    loaded = (
        node_feats, edge_feats, senders[None, :], receivers[None, :], w_edge_in, w_edge_out,
        gain_edge[None, :], w_node_in, w_node_out, gain_node[None, :], d_nodes_out, d_edges_out,
    )
    scratch = [
        *[pltpu.VMEM(a.shape, a.dtype) for a in loaded],
        dma((len(loaded),)),
        pltpu.VMEM((4, shard, width), BF16),
        pltpu.VMEM((6 * shard, width), BF16),
        pltpu.VMEM((edges, 8), jnp.int32),
        pltpu.VMEM((edges, width), F32),
        pltpu.VMEM((edges, width), F32),
        pltpu.VMEM((edges, 1), F32),
        pltpu.VMEM((edges, width), BF16),
        pltpu.VMEM((2, shard, width), F32),
        pltpu.VMEM((shard, width), F32),
        pltpu.VMEM((2, shard, width), BF16),
        pltpu.VMEM((4 * shard, width), F32),
        pltpu.VMEM((2 * shard, width), F32),
        pltpu.VMEM((width, width), F32),
        pltpu.VMEM((width, width), F32),
        pltpu.VMEM((rows_e, width), F32),
        pltpu.VMEM((rows_n, width), F32),
        pltpu.VMEM((2, shard, width), BF16),
        pltpu.VMEM((2, shard, width), BF16),
        pltpu.VMEM((2, shard, width), F32),
        pltpu.VMEM((shard, width), F32),
        pltpu.VMEM((len(digits) + 2, 8, width), F32),
        pltpu.VMEM((1 + partners, 8, width), F32),
        pltpu.VMEM((edges, width), BF16),
        *bufs_n,
        *bufs_e,
        dma((12,)), dma((12,)),
        dma((copies,)), dma((copies,)), dma((copies,)), dma((copies,)),
        dma((1 + partners,)), dma((1 + partners,)),
        *levels_n,
        *levels_e,
    ]
    big = [jax.ShapeDtypeStruct((n, width), BF16) for n in (shard, edges, shard, edges)]
    held = pl.pallas_call(
        functools.partial(kernel, digits, n_row, chunk),
        out_shape=(*big, gathered_e, gathered_n, jax.ShapeDtypeStruct((8, width), F32)),
        in_specs=[hbm] * 4 + [smem] + [hbm] * 8,
        out_specs=tuple([vmem] * 7),
        scratch_shapes=scratch,
        compiler_params=pltpu.CompilerParams(
            collective_id=0, has_side_effects=True, vmem_limit_bytes=60 * 2**20
        ),
        name="layer",
    )(
        *loaded[:4], edge_count, *loaded[4:],
    )
    flat = jax.ShapeDtypeStruct((1, width), F32)
    out = pl.pallas_call(
        unpack,
        out_shape=(
            *big,
            jax.ShapeDtypeStruct(w_edge_in.shape, BF16),
            jax.ShapeDtypeStruct(w_edge_out.shape, BF16),
            flat,
            jax.ShapeDtypeStruct(w_node_in.shape, BF16),
            jax.ShapeDtypeStruct(w_node_out.shape, BF16),
            flat,
        ),
        in_specs=[hbm] * 7,
        out_specs=tuple([hbm] * 4 + [vmem] * 6),
        scratch_shapes=[pltpu.VMEM(a.shape, a.dtype) for a in held] + [dma((7,)), dma((4,))],
        compiler_params=pltpu.CompilerParams(vmem_limit_bytes=60 * 2**20),
        name="unpack",
    )(*held)
    return (*out[:6], out[6][0], *out[7:9], out[9][0])


def padded(x, sides, width):
    for axis, dim in sides:
        devices, length = (lax.axis_size(axis), x.shape[dim])
        up = [(i, (i + 1) % devices) for i in range(devices - 1)]
        down = [(j, i) for i, j in up]
        last = lax.slice_in_dim(x, length - width, length, axis=dim)
        first = lax.slice_in_dim(x, 0, width, axis=dim)
        before = lax.ppermute(last, axis, up)
        after = lax.ppermute(first, axis, down)
        x = jnp.concatenate([before, x, after], axis=dim)
    return x


def from_behind(value, axis, steps):
    count = lax.axis_size(axis)
    first, last = (max(0, -steps), min(count, count - steps))
    return lax.ppermute(value, axis, [(source, source + steps) for source in range(first, last)])


def plain_slope(pre):
    sigmoid = jax.nn.sigmoid(pre)
    return sigmoid * (1.0 + pre * (1.0 - sigmoid))


def plain_norm(values):
    centred = values - jnp.mean(values, axis=-1, keepdims=True)
    inv_scale = lax.rsqrt(jnp.mean(centred * centred, axis=-1, keepdims=True) + 1e-05)
    return (centred * inv_scale, inv_scale)


def plain_back(upstream, normed, inv_scale):
    return inv_scale * (
        upstream
        - jnp.mean(upstream, axis=-1, keepdims=True)
        - normed * jnp.mean(upstream * normed, axis=-1, keepdims=True)
    )


def plain_rows(left, right):
    return lax.dot_general(
        left, right, (((0,), (0,)), ((), ())), preferred_element_type=jnp.float32
    )


def plain_times(left, right):
    return lax.dot_general(
        left, right, (((1,), (1,)), ((), ())), preferred_element_type=jnp.float32
    )


def plain(
    node_feats,
    edge_feats,
    senders,
    receivers,
    edge_count,
    w_edge_in,
    w_edge_out,
    gain_edge,
    w_node_in,
    w_node_out,
    gain_node,
    d_nodes_out,
    d_edges_out,
):
    width = node_feats.shape[1]
    edge_rows = edge_feats.shape[0]
    grouped = lax.all_gather(node_feats, "rep", axis=0, tiled=True)
    group_rows = grouped.shape[0]
    rim_rows = group_rows // 2
    extended = padded(grouped, (("row", 0),), rim_rows)
    group_start = lax.axis_index("row") * group_rows
    recv_local = receivers - group_start
    send_local = senders - group_start + rim_rows
    slots = jnp.arange(edge_rows, dtype=jnp.int32)
    live_mask = (slots < edge_count[0]).astype(jnp.float32)[:, None]
    edge_input = jnp.concatenate(
        [edge_feats, jnp.take(extended, send_local, axis=0), jnp.take(grouped, recv_local, axis=0)],
        axis=1,
    )
    edge_pre = jnp.dot(edge_input, w_edge_in, preferred_element_type=jnp.float32)
    edge_act = jax.nn.silu(edge_pre).astype(jnp.bfloat16)
    edge_mix = jnp.dot(edge_act, w_edge_out, preferred_element_type=jnp.float32)
    edge_norm, edge_scale = plain_norm(edge_mix)
    message = live_mask * edge_norm * gain_edge
    edges_out = (edge_feats.astype(jnp.float32) + message).astype(jnp.bfloat16)
    message_b = message.astype(jnp.bfloat16)
    recv_table = (
        lax.broadcasted_iota(jnp.int32, (group_rows, edge_rows), 0) == recv_local[None, :]
    ).astype(jnp.bfloat16)
    partial_sums = jnp.dot(recv_table, message_b, preferred_element_type=jnp.float32)
    aggregate = lax.psum_scatter(partial_sums, "rep", scatter_dimension=0, tiled=True)
    node_input = jnp.concatenate([node_feats, aggregate.astype(jnp.bfloat16)], axis=1)
    node_pre = jnp.dot(node_input, w_node_in, preferred_element_type=jnp.float32)
    node_act = jax.nn.silu(node_pre).astype(jnp.bfloat16)
    node_mix = jnp.dot(node_act, w_node_out, preferred_element_type=jnp.float32)
    node_norm, node_scale = plain_norm(node_mix)
    nodes_out = (node_feats.astype(jnp.float32) + node_norm * gain_node).astype(jnp.bfloat16)
    grad_nodes = d_nodes_out.astype(jnp.float32)
    d_gain_node = jnp.sum(grad_nodes * node_norm, axis=0)
    d_node_mix = plain_back(grad_nodes * gain_node, node_norm, node_scale).astype(jnp.bfloat16)
    d_w_node_out = plain_rows(node_act, d_node_mix)
    d_node_pre = (plain_times(d_node_mix, w_node_out) * plain_slope(node_pre)).astype(
        jnp.bfloat16
    )
    d_w_node_in = plain_rows(node_input, d_node_pre)
    d_node_input = plain_times(d_node_pre, w_node_in)
    d_aggregate = d_node_input[:, width:].astype(jnp.bfloat16)
    d_direct = grad_nodes + d_node_input[:, :width]
    group_grad = lax.all_gather(d_aggregate, "rep", axis=0, tiled=True)
    d_message = live_mask * (
        d_edges_out.astype(jnp.float32)
        + jnp.take(group_grad, recv_local, axis=0).astype(jnp.float32)
    )
    d_gain_edge = jnp.sum(d_message * edge_norm, axis=0)
    d_edge_mix = plain_back(d_message * gain_edge, edge_norm, edge_scale).astype(jnp.bfloat16)
    d_w_edge_out = plain_rows(edge_act, d_edge_mix)
    d_edge_pre = (plain_times(d_edge_mix, w_edge_out) * plain_slope(edge_pre)).astype(
        jnp.bfloat16
    )
    d_w_edge_in = plain_rows(edge_input, d_edge_pre)
    d_edge_input = plain_times(d_edge_pre, w_edge_in)
    d_edges = (d_edges_out.astype(jnp.float32) + d_edge_input[:, :width]).astype(jnp.bfloat16)
    d_sender = d_edge_input[:, width : 2 * width].astype(jnp.bfloat16)
    d_receiver = d_edge_input[:, 2 * width :].astype(jnp.bfloat16)
    send_table = (
        lax.broadcasted_iota(jnp.int32, (group_rows + 2 * rim_rows, edge_rows), 0)
        == send_local[None, :]
    ).astype(jnp.bfloat16)
    send_sums = jnp.dot(send_table, d_sender, preferred_element_type=jnp.float32)
    recv_sums = jnp.dot(recv_table, d_receiver, preferred_element_type=jnp.float32)
    from_next = from_behind(send_sums[:rim_rows].astype(jnp.bfloat16), "row", -1).astype(
        jnp.float32
    )
    from_prev = from_behind(
        send_sums[group_rows + rim_rows :].astype(jnp.bfloat16), "row", 1
    ).astype(jnp.float32)
    inner = send_sums[rim_rows : rim_rows + group_rows]
    inner = jnp.concatenate([inner[:rim_rows] + from_prev, inner[rim_rows:] + from_next], axis=0)
    edge_terms = lax.psum_scatter(
        inner.astype(jnp.bfloat16), "rep", scatter_dimension=0, tiled=True
    ).astype(jnp.float32) + lax.psum_scatter(
        recv_sums.astype(jnp.bfloat16), "rep", scatter_dimension=0, tiled=True
    ).astype(
        jnp.float32
    )
    d_nodes = (d_direct + edge_terms).astype(jnp.bfloat16)
    summed = lax.psum(
        (d_w_edge_in, d_w_edge_out, d_gain_edge, d_w_node_in, d_w_node_out, d_gain_node),
        ("row", "rep"),
    )
    return (
        nodes_out,
        edges_out,
        d_nodes,
        d_edges,
        summed[0].astype(jnp.bfloat16),
        summed[1].astype(jnp.bfloat16),
        summed[2],
        summed[3].astype(jnp.bfloat16),
        summed[4].astype(jnp.bfloat16),
        summed[5],
    )


def solution(mesh):
    split, flat, whole = P(("row", "rep"), None), P(("row", "rep")), P()
    layer = functools.partial(local, mesh.shape["row"]) if mesh.shape["rep"] == 2 else plain
    return jax.shard_map(
        layer,
        mesh=mesh,
        in_specs=(split, split, flat, flat, flat) + (whole,) * 6 + (split, split),
        out_specs=(split,) * 4 + (whole,) * 6,
        check_vma=False,
    )
```
